768 devices in a mesh: fsdp: 48 (over y_lo, z, core), frame: 16 (over x, y_hi).
Axes of the slice: x: 4, y: 8 (y_hi: 4, y_lo: 2; y = y_hi * 2 + y_lo), z: 12, core: 2. Of those that a mesh axis runs over, the one named last changes fastest.
Arguments:
- frames: bfloat16 [48, 6144, 3072], P('fsdp', 'frame'), may hold values from -6 to 6
- modulation: float32 [48, 2, 3072], P('fsdp'), may hold values from -3 to 3
- w_qkv: bfloat16 [3072, 768], P('fsdp'), may hold values from -0.109375 to 0.109375
- qk_gain: float32 [2, 128], replicated, may hold values from 0.1 to 1.9
- w_out: bfloat16 [256, 3072], P(None, 'fsdp'), may hold values from -0.375 to 0.375
Outputs:
- mixed: bfloat16 [48, 6144, 3072], P('fsdp', 'frame')
The draws below stay inside these ranges and needn't reach their ends.
All inputs are finite; a program needn't handle non-finite values.
Results may differ from the reference program's by a relative error of at most 0.0053.
Values may be sent and summed in bfloat16 or wider, within the bound.
A program may use at most 64 MiB of HBM per device.

```python
import math
import jax
import jax.numpy as jnp
from jax import lax

D = 3072
HEAD_DIM = 128
HEADS = 2
TILE = 128
REACH = 2
BORDER = 256
WINDOW = 640
VIDEOS = 48
FRAME_TOK = 6144
TILES = 48


def block_scale(stream_key, shape, split, low, high):
    loudness = 1.0
    for dim, blocks in split:
        heights = jax.random.uniform(jax.random.fold_in(jax.random.fold_in(stream_key, 6), dim), (blocks,), jnp.float32, low / len(split), high / len(split))
        loudness = loudness * jnp.repeat(jnp.exp(heights), shape[dim] // blocks).reshape((-1,) + (1,) * (len(shape) - 1 - dim))
    return loudness


def normal_values(key, extent, deviation, bound, cuts=(), kind=jnp.bfloat16):
    factor_of = block_scale(key, extent, cuts, -0.22, 0.18) if cuts else 1.0
    array = jax.random.normal(key, extent, jnp.float32) * deviation * factor_of
    return jnp.minimum(jnp.maximum(array, -bound), bound).astype(kind)


def setup_inputs(seed: int = 0) -> dict:
    splits = jax.random.split(jax.random.key(seed), 6)
    return {
        "frames": normal_values(splits[0], (VIDEOS, FRAME_TOK, D), 1.0, 6.0, ((0, 48), (1, 16))),
        "modulation": normal_values(splits[1], (VIDEOS, 2, D), 0.5, 3.0, ((0, 48),), jnp.float32),
        "w_qkv": normal_values(splits[2], (D, 3 * HEADS * HEAD_DIM), D ** -0.5, 0.109375, ((0, 48),)),
        "qk_gain": jnp.clip(1.0 + 0.18 * jax.random.normal(splits[3], (2, HEAD_DIM), jnp.float32), 0.1, 1.9),
        "w_out": normal_values(splits[4], (HEADS * HEAD_DIM, D), (HEADS * HEAD_DIM) ** -0.5, 0.375, ((1, 48),)),
    }


def norm_rows(frames_rows, modulation_rows):
    values_full = frames_rows.astype(jnp.float32)
    average = lax.optimization_barrier(jnp.mean(values_full, axis=-1, keepdims=True))
    centered = values_full - average
    spread = lax.optimization_barrier(jnp.mean(centered * centered, axis=-1, keepdims=True))
    normed = centered * lax.rsqrt(spread + 1e-06)
    return (normed * (1.0 + modulation_rows[0]) + modulation_rows[1]).astype(jnp.bfloat16)

def head_norm(projected, gain_row):
    count = projected.shape[0]
    shaped = projected.reshape(count, HEADS, HEAD_DIM)
    squares = lax.optimization_barrier(jnp.mean(shaped * shaped, axis=-1, keepdims=True))
    scaled = shaped * lax.rsqrt(squares + 1e-06) * gain_row
    return scaled.reshape(count, HEADS * HEAD_DIM).astype(jnp.bfloat16)

def reference(frames, modulation, w_qkv, qk_gain, w_out):
    width = HEADS * HEAD_DIM
    scale_factor = 1.0 / math.sqrt(HEAD_DIM)

    def attend_video(inputs):
        frames_video, modulation_video = inputs
        normed = norm_rows(frames_video, modulation_video)
        projected = jnp.dot(normed, w_qkv, preferred_element_type=jnp.float32)
        queries = head_norm(projected[:, :width], qk_gain[0])
        key_part = head_norm(projected[:, width:2 * width], qk_gain[1])
        value_part = projected[:, 2 * width:].astype(jnp.bfloat16)
        stacked = jnp.concatenate([key_part, value_part], axis=1)
        padded = jnp.pad(stacked, ((BORDER, BORDER), (0, 0)))

        def one_tile(tile_index):
            first_tile = tile_index - REACH
            query_tile = lax.dynamic_slice_in_dim(queries, (tile_index * TILE).astype(jnp.int32), TILE, 0)
            query_tile = query_tile.reshape(TILE, HEADS, HEAD_DIM).astype(jnp.float32)
            window = lax.dynamic_slice_in_dim(padded, (first_tile * TILE + BORDER).astype(jnp.int32), WINDOW, 0)
            positions = first_tile * TILE + jnp.arange(WINDOW, dtype=jnp.int32)
            inside = (positions >= 0) & (positions < FRAME_TOK)
            key_win = window[:, :width].reshape(WINDOW, HEADS, HEAD_DIM).astype(jnp.float32)
            value_win = window[:, width:].reshape(WINDOW, HEADS, HEAD_DIM).astype(jnp.float32)
            scores = jnp.einsum('qhd,khd->hqk', query_tile, key_win) * scale_factor
            raised = jnp.where(inside[None, None, :], jnp.exp(scores), 0.0)
            probs = (raised / lax.optimization_barrier(jnp.sum(raised, axis=-1, keepdims=True))).astype(jnp.bfloat16)
            return jnp.einsum('hqk,khd->qhd', probs.astype(jnp.float32), value_win).astype(jnp.bfloat16)
        attended = lax.map(one_tile, jnp.arange(TILES, dtype=jnp.int32)).reshape(FRAME_TOK, width)
        return jnp.dot(attended, w_out, preferred_element_type=jnp.float32).astype(jnp.bfloat16)
    return lax.map(attend_video, (frames, modulation))
```

```python
import functools
import math

import jax
import jax.numpy as jnp
from jax import lax
from jax.experimental import pallas as pl
from jax.experimental.pallas import tpu as pltpu
from jax.sharding import Mesh
from jax.sharding import PartitionSpec as P

HEAD_DIM = 128
HEADS = 2
TILE = 128
BORDER = 256
WIDTH = HEADS * HEAD_DIM
ROWS = 64
MESH = pl.DeviceIdType.MESH
AXES = ("yl", "z", "c", "x", "yh")
KEY, VALUE, QUERY, OUT = 0, 1, 2, 3
NORM_ROWS = 16


class Counter:
    def __init__(self):
        self.ids = {}

    def __call__(self, *key):
        return self.ids.setdefault(key, len(self.ids))


def head_norm(block, gain):
    parts = []
    for head in range(HEADS):
        part = block[:, head * HEAD_DIM : (head + 1) * HEAD_DIM]
        squares = jnp.mean(part * part, axis=-1, keepdims=True)
        parts.append(part * lax.rsqrt(squares + 1e-06) * gain)
    return jnp.concatenate(parts, axis=1).astype(jnp.bfloat16)


def kernel(
    sizes,
    copies,
    frames,
    modulation,
    w_qkv,
    qk_gain,
    w_out,
    attended,
    out_rows,
    weights,
    raw,
    normed,
    mod,
    gain,
    w_out_here,
    acc,
    padded,
    query,
    top,
    bottom,
    local_sems,
    send_sems,
    recv_sems,
):
    n, nx, nyh = sizes
    half = n // 2
    rows = raw.shape[0]
    tiles = rows // TILE
    yl, z, c = lax.axis_index("yl"), lax.axis_index("z"), lax.axis_index("c")
    x, yh = lax.axis_index("x"), lax.axis_index("yh")
    other = 1 - yl
    frame = x * nyh + yh
    z_next = [{"z": lax.rem(z + 1, n)}, {"z": lax.rem(z + n - 1, n)}]
    y_next = [
        {"yl": other, "yh": lax.rem(yh + yl, nyh)},
        {"yl": other, "yh": lax.rem(yh + nyh - other, nyh)},
    ]
    sibling = {"c": 1 - c}
    after = {"yh": lax.rem(yh + 1, nyh), "x": lax.rem(x + (yh + 1) // nyh, nx)}
    before = {
        "yh": lax.rem(yh + nyh - 1, nyh),
        "x": lax.rem(x + nx - 1 + (yh + nyh - 1) // nyh, nx),
    }

    def far(d, s):
        return lax.rem(z + n + (-s if d == 0 else s), n)

    def local(src, dst, i):
        copy = pltpu.make_async_copy(src, dst, local_sems.at[i])
        copy.start()
        return copy

    own = weights.at[yl, z, c]
    loads = [
        local(w_qkv.at[:, WIDTH : 2 * WIDTH], own.at[KEY], 0),
        local(w_qkv.at[:, 2 * WIDTH :], own.at[VALUE], 1),
        local(w_qkv.at[:, :WIDTH], own.at[QUERY], 2),
        local(w_out, w_out_here, 3),
        local(modulation, mod, 4),
        local(qk_gain, gain, 5),
        local(frames, raw, 6),
    ]

    sent = []

    def remote(src, dst, to, *key):
        i = copies(*key)
        return pltpu.make_async_remote_copy(
            src, dst, send_sems.at[i], recv_sems.at[i], device_id=to, device_id_type=MESH
        )

    def send(ref, to, *key, dst=None):
        copy = remote(ref, ref if dst is None else dst, to, *key)
        copy.start()
        sent.append(copy)

    def arrived(ref, to, *key):
        remote(ref, ref, to, *key).wait_recv()

    barrier = pltpu.get_barrier_semaphore()
    for to in (*z_next, *y_next, sibling, after, before):
        pl.semaphore_signal(barrier, inc=1, device_id=to, device_id_type=MESH)
    pl.semaphore_wait(barrier, 7)

    def kv(row, d, s):
        return weights.at[row, far(d, s), c]

    loads[0].wait()
    loads[1].wait()
    for u in (0, 1):
        for d in (0, 1):
            send(own.at[u], z_next[d], "kv z", u, d, 1)
    for d in (0, 1):
        send(own.at[d], y_next[d], "kv y", d, d, 0)
    send(own.at[0:2], sibling, "kv s", 0, 0, 0)
    loads[2].wait()
    send(own.at[QUERY], y_next[0], "q y")
    send(own.at[QUERY], sibling, "q s own")

    loads[3].wait()
    own[OUT] = w_out_here[...].astype(jnp.float32).T.astype(jnp.bfloat16)

    loads[4].wait()
    loads[5].wait()
    loads[6].wait()

    def norm_step(i, carry):
        at = pl.ds(pl.multiple_of(i * NORM_ROWS, NORM_ROWS), NORM_ROWS)
        full = raw[at, :].astype(jnp.float32)
        centered = full - jnp.mean(full, axis=-1, keepdims=True)
        spread = jnp.mean(centered * centered, axis=-1, keepdims=True)
        scaled = centered * lax.rsqrt(spread + 1e-06)
        normed[at, :] = (scaled * (1.0 + mod[0:1, :]) + mod[1:2, :]).astype(jnp.bfloat16)
        return carry

    lax.fori_loop(0, rows // NORM_ROWS, norm_step, 0)
    send(own.at[OUT], y_next[1], "o y")
    send(own.at[OUT], sibling, "o s own")

    def from_core(row, d, s):
        kind = "kv s" if row is yl else "kv t"
        if s == 0 and row is yl:
            arrived(weights.at[yl, z, 1 - c, 0:2], sibling, kind, 0, 0, 0)
        elif s in (0, half):
            arrived(weights.at[row, far(d, s), 1 - c, d], sibling, kind, d, s)
        else:
            arrived(weights.at[row, far(d, s), 1 - c, 0:2], sibling, kind, d, s)

    def shards(row, s):
        for d in (0, 1):
            if not (s == 0 and row is yl and d == 1):
                from_core(row, d, s)
        return [(row, far(d, s)) for d in ((0,) if s in (0, half) else (0, 1))]

    def accumulate(first, places):
        lhs = jnp.concatenate(
            [
                normed[:, pl.ds(pl.multiple_of((row * n + at) * 2 * ROWS, 2 * ROWS), 2 * ROWS)]
                for row, at in places
            ],
            axis=1,
        )
        for u in (KEY, VALUE):
            rhs = jnp.concatenate(
                [weights[row, at, :, u].reshape(2 * ROWS, WIDTH) for row, at in places], axis=0
            )
            part = jnp.dot(lhs, rhs, preferred_element_type=jnp.float32)
            if first:
                acc[:, u * WIDTH : (u + 1) * WIDTH] = part
            else:
                acc[:, u * WIDTH : (u + 1) * WIDTH] += part

    def across(s):
        for d in (0, 1):
            for u in (0, 1):
                if s in (0, half) and u != d:
                    continue
                arrived(kv(other, d, s).at[u], y_next[1 - d], "kv y", u, d, s)
            ref = kv(other, d, s)
            send(ref.at[d] if s in (0, half) else ref.at[0:2], sibling, "kv t", d, s)

    places = []
    for s in range(1, half + 1):
        for u in (0, 1):
            for d in (0, 1):
                if s == half and u != d:
                    continue
                ref = kv(yl, d, s)
                arrived(ref.at[u], z_next[1 - d], "kv z", u, d, s)
                if s < half - 1 or (s == half - 1 and u == d):
                    send(ref.at[u], z_next[d], "kv z", u, d, s + 1)
                send(ref.at[u], y_next[d], "kv y", u, d, s)
        for d in (0, 1):
            ref = kv(yl, d, s)
            send(ref.at[d] if s == half else ref.at[0:2], sibling, "kv s", d, s)
        if s == half - 1:
            start_ring = True
            arrived(weights.at[other, z, c, QUERY], y_next[1], "q y")
            for d in (0, 1):
                send(weights.at[yl, z, c, QUERY], z_next[d], "q z", 0, d, 1)
            for d in (0, 1):
                send(weights.at[other, z, c, QUERY], z_next[d], "q z", 1, d, 1)
            send(weights.at[other, z, c, QUERY], sibling, "q s other")
        across(s - 1)
        places += shards(yl, s - 1)
        if s >= 2:
            places += shards(other, s - 2)
            accumulate(s == 2, places)
            places = []
    across(half)
    places = shards(yl, half) + shards(other, half - 1) + shards(other, half)
    accumulate(False, places)

    padded[BORDER : BORDER + rows, :WIDTH] = head_norm(acc[:, :WIDTH], gain[1:2, :])
    padded[BORDER : BORDER + rows, WIDTH:] = acc[:, WIDTH:].astype(jnp.bfloat16)
    send(
        padded.at[BORDER : 2 * BORDER],
        before,
        "head",
        dst=padded.at[BORDER + rows : 2 * BORDER + rows],
    )
    send(padded.at[rows : rows + BORDER], after, "tail", dst=padded.at[0:BORDER])

    def ring_step(name, b, s):
        for u in (0, 1):
            row = yl if u == 0 else other
            for d in (0, 1):
                if s == half and u != d:
                    continue
                ref = weights.at[row, far(d, s), c, b]
                arrived(ref, z_next[1 - d], name + " z", u, d, s)
                if s < half - 1 or (s == half - 1 and u == d):
                    send(ref, z_next[d], name + " z", u, d, s + 1)
                send(ref, sibling, name + " s", u, d, s)

    def ring_end(name, b):
        arrived(weights.at[yl, z, 1 - c, b], sibling, name + " s own")
        arrived(weights.at[other, z, 1 - c, b], sibling, name + " s other")
        for s in range(1, half + 1):
            for u in (0, 1):
                row = yl if u == 0 else other
                for d in (0, 1):
                    if s == half and u != d:
                        continue
                    arrived(weights.at[row, far(d, s), 1 - c, b], sibling, name + " s", u, d, s)

    def project_queries():
        depth = 8 * ROWS
        steps = n // 4

        def step(k, carry):
            lhs = normed[:, pl.ds(pl.multiple_of(k * depth, depth), depth)]
            rhs = weights[k // steps, pl.ds(lax.rem(k, steps) * 4, 4), :, QUERY]
            part = jnp.dot(lhs, rhs.reshape(depth, WIDTH), preferred_element_type=jnp.float32)
            return carry + part

        total = lax.fori_loop(0, 2 * steps, step, jnp.zeros((rows, WIDTH), jnp.float32))
        query[...] = head_norm(total, gain[0:1, :])

    scale = 1.0 / math.sqrt(HEAD_DIM)

    def part_of(tile, head, start, count, weight=None):
        cols = slice(head * HEAD_DIM, (head + 1) * HEAD_DIM)
        q = query[tile * TILE : (tile + 1) * TILE, cols]
        k = padded[start : start + count, cols]
        v = padded[start : start + count, WIDTH + head * HEAD_DIM : WIDTH + (head + 1) * HEAD_DIM]
        score = lax.dot_general(
            q, k, (((1,), (1,)), ((), ())), preferred_element_type=jnp.float32
        )
        raised = jnp.exp(score * scale)
        if weight is not None:
            raised = raised * weight
        low = jnp.sum(raised, axis=-1, keepdims=True)
        high = jnp.dot(raised.astype(jnp.bfloat16), v, preferred_element_type=jnp.float32)
        return high, jnp.broadcast_to(low, (TILE, HEAD_DIM))

    def near_part(tile):
        for head in range(HEADS):
            high, low = part_of(tile, head, BORDER, rows)
            top[tile, head] = high
            bottom[tile, head] = low

    for s in range(1, half + 1):
        ring_step("q", QUERY, s)
        if s == half - 1:
            arrived(weights.at[other, z, c, OUT], y_next[0], "o y")
            for d in (0, 1):
                send(weights.at[yl, z, c, OUT], z_next[d], "o z", 0, d, 1)
            for d in (0, 1):
                send(weights.at[other, z, c, OUT], z_next[d], "o z", 1, d, 1)
            send(weights.at[other, z, c, OUT], sibling, "o s other")
    for s in range(1, half + 1):
        ring_step("o", OUT, s)
        if s == 1:
            ring_end("q", QUERY)
            project_queries()
        if s == 2:
            near_part(0)
        if s == min(3, half):
            near_part(1)
        if s == min(4, half):
            near_part(2)
    ring_end("o", OUT)
    stored = local(weights.at[:, :, :, OUT], out_rows, 0)

    arrived(padded.at[0:BORDER], before, "tail")
    arrived(padded.at[BORDER + rows : 2 * BORDER + rows], after, "head")
    has_before = jnp.where(frame > 0, 1.0, 0.0)
    has_after = jnp.where(frame < nx * nyh - 1, 1.0, 0.0)
    for tile in range(tiles):
        done = []
        for head in range(HEADS):
            high, low = top[tile, head], bottom[tile, head]
            first, last = tile * TILE, (tile + 5) * TILE
            if first < BORDER:
                more, less = part_of(tile, head, first, BORDER - first, has_before)
                high, low = high + more, low + less
            if last > BORDER + rows:
                more, less = part_of(tile, head, BORDER + rows, last - BORDER - rows, has_after)
                high, low = high + more, low + less
            done.append((high / low).astype(jnp.bfloat16))
        attended[tile * TILE : (tile + 1) * TILE, :] = jnp.concatenate(done, axis=1)
    stored.wait()
    for copy in sent:
        copy.wait_send()


def on_device(sizes, frames, modulation, w_qkv, qk_gain, w_out):
    n = sizes[0]
    rows, features = frames.shape[1:]
    copies = Counter()
    anywhere = pl.BlockSpec(memory_space=pl.ANY)
    attended, out_rows = pl.pallas_call(
        functools.partial(kernel, sizes, copies),
        out_shape=(
            jax.ShapeDtypeStruct((rows, WIDTH), jnp.bfloat16),
            jax.ShapeDtypeStruct((2, n, 2, ROWS, WIDTH), jnp.bfloat16),
        ),
        in_specs=[anywhere] * 5,
        out_specs=(pl.BlockSpec(memory_space=pltpu.VMEM), anywhere),
        scratch_shapes=[
            pltpu.VMEM((2, n, 2, 4, ROWS, WIDTH), jnp.bfloat16),
            pltpu.VMEM((rows, features), jnp.bfloat16),
            pltpu.VMEM((rows, features), jnp.bfloat16),
            pltpu.VMEM((2, features), jnp.float32),
            pltpu.VMEM((2, HEAD_DIM), jnp.float32),
            pltpu.VMEM((WIDTH, ROWS), jnp.bfloat16),
            pltpu.VMEM((rows, 2 * WIDTH), jnp.float32),
            pltpu.VMEM((rows + 2 * BORDER, 2 * WIDTH), jnp.bfloat16),
            pltpu.VMEM((rows, WIDTH), jnp.bfloat16),
            pltpu.VMEM((rows // TILE, HEADS, TILE, HEAD_DIM), jnp.float32),
            pltpu.VMEM((rows // TILE, HEADS, TILE, HEAD_DIM), jnp.float32),
            pltpu.SemaphoreType.DMA((7,)),
            pltpu.SemaphoreType.DMA((220,)),
            pltpu.SemaphoreType.DMA((220,)),
        ],
        compiler_params=pltpu.CompilerParams(collective_id=0, has_side_effects=True),
    )(frames[0], modulation[0], w_qkv, qk_gain, w_out)
    mixed = lax.dot_general(
        attended,
        out_rows.reshape(features, WIDTH),
        (((1,), (1,)), ((), ())),
        preferred_element_type=jnp.float32,
    ).astype(jnp.bfloat16)
    return mixed[None]


def solution(mesh, n=12, nx=4, nyh=4):
    finer = Mesh(mesh.devices.reshape(2, n, 2, nx, nyh), AXES)
    fsdp, frame = ("yl", "z", "c"), ("x", "yh")
    placed = (P(fsdp, frame, None), P(fsdp, None, None), P(fsdp, None), P(), P(None, fsdp))
    return jax.shard_map(
        functools.partial(on_device, (n, nx, nyh)),
        mesh=finer,
        in_specs=placed,
        out_specs=P(fsdp, frame, None),
        check_vma=False,
    )
```

```python
import functools
import math

import jax
import jax.numpy as jnp
from jax import lax
from jax.experimental import pallas as pl
from jax.experimental.pallas import tpu as pltpu
from jax.sharding import Mesh
from jax.sharding import PartitionSpec as P

HEAD_DIM = 128
HEADS = 2
TILE = 128
BORDER = 256
WIDTH = HEADS * HEAD_DIM
ROWS = 64
MESH = pl.DeviceIdType.MESH
AXES = ("yl", "z", "c", "x", "yh")
KEY, VALUE = 0, 1
QUERY, OUT = 0, 1
PARTS = 4
PIECE = ROWS // PARTS
NORM_ROWS = 16


class Counter:
    def __init__(self):
        self.ids = {}

    def __call__(self, *key):
        return self.ids.setdefault(key, len(self.ids))


def head_norm(block, gain):
    parts = []
    for head in range(HEADS):
        part = block[:, head * HEAD_DIM : (head + 1) * HEAD_DIM]
        squares = jnp.mean(part * part, axis=-1, keepdims=True)
        parts.append(part * lax.rsqrt(squares + 1e-06) * gain)
    return jnp.concatenate(parts, axis=1).astype(jnp.bfloat16)


def stage_slots(half):
    bounds = [0, 5] if half > 2 else [0, 4]
    while bounds[-1] < 2 * half:
        bounds.append(min(bounds[-1] + 4, 2 * half))
    return list(zip(bounds[:-1], bounds[1:]))


def kernel(
    sizes,
    copies,
    frames,
    modulation,
    w_qkv,
    qk_gain,
    w_out_t,
    mixed,
    kv_weights,
    qo_weights,
    raw,
    normed,
    mod,
    gain,
    acc,
    padded,
    query,
    top,
    bottom,
    attended,
    result,
    local_sems,
    send_sems,
    recv_sems,
    out_sems,
):
    n, nx, nyh = sizes
    half = n // 2
    stages = half // 2
    slots = stage_slots(half)
    rows = raw.shape[0]
    tiles = rows // TILE
    yl, z, c = lax.axis_index("yl"), lax.axis_index("z"), lax.axis_index("c")
    x, yh = lax.axis_index("x"), lax.axis_index("yh")
    other = 1 - yl
    frame = x * nyh + yh

    def z_by(d, t):
        return {"z": lax.rem(z + (t if d == 0 else n - t), n)}

    y_next = [
        {"yl": other, "yh": lax.rem(yh + yl, nyh)},
        {"yl": other, "yh": lax.rem(yh + nyh - other, nyh)},
    ]
    x_at = [lax.rem(x + 1, nx), lax.rem(x + nx - 1, nx)]
    x_next = [{"x": x_at[0]}, {"x": x_at[1]}]
    x_far = lax.rem(x + 2, nx)
    sibling = {"c": 1 - c}
    after = {"yh": lax.rem(yh + 1, nyh), "x": lax.rem(x + (yh + 1) // nyh, nx)}
    before = {
        "yh": lax.rem(yh + nyh - 1, nyh),
        "x": lax.rem(x + nx - 1 + (yh + nyh - 1) // nyh, nx),
    }

    def slot(d, s):
        if s == 0:
            return 0
        base = 1 + 4 * ((s - 1) // 2)
        if s >= half - 1:
            return base + (d if s < half else 2)
        return base + 2 * d + (s - 1) % 2

    offset = {0: 0}
    for d in (0, 1):
        for s in range(1, half + 1):
            offset[slot(d, s)] = -s if d == 0 else s

    def column(row, at):
        start = ((yl if row == 0 else other) * n + lax.rem(z + n + offset[at], n)) * 2 * ROWS
        return pl.ds(pl.multiple_of(start, 2 * ROWS), 2 * ROWS)

    def local(src, dst, i):
        copy = pltpu.make_async_copy(src, dst, local_sems.at[i])
        copy.start()
        return copy

    piece = pl.ds(pl.multiple_of(x * PIECE, PIECE), PIECE)
    loads = [
        local(w_qkv.at[:, WIDTH : 2 * WIDTH], kv_weights.at[c, 0, 0, KEY], 0),
        local(w_qkv.at[:, 2 * WIDTH :], kv_weights.at[c, 0, 0, VALUE], 1),
        local(w_qkv.at[piece, :WIDTH], qo_weights.at[x, c, 0, 0, QUERY], 2),
        local(w_out_t.at[piece, :], qo_weights.at[x, c, 0, 0, OUT], 3),
        local(modulation, mod, 4),
        local(qk_gain, gain, 5),
        local(frames, raw, 6),
    ]

    sent = []

    def remote(src, dst, to, *key):
        i = copies(*key)
        return pltpu.make_async_remote_copy(
            src, dst, send_sems.at[i], recv_sems.at[i], device_id=to, device_id_type=MESH
        )

    def send(ref, to, *key, dst=None):
        copy = remote(ref, ref if dst is None else dst, to, *key)
        copy.start()
        sent.append(copy)

    def arrived(ref, to, *key):
        remote(ref, ref, to, *key).wait_recv()

    barrier = pltpu.get_barrier_semaphore()
    partners = [z_by(d, t) for d in (0, 1) for t in (1, 2)]
    partners += [*y_next, *x_next, sibling, after, before]
    for to in partners:
        pl.semaphore_signal(barrier, inc=1, device_id=to, device_id_type=MESH)
    pl.semaphore_wait(barrier, len(partners))

    def kv_at(u, d, s):
        return kv_weights.at[c, 0, slot(d, s), u]

    def kv_pass(u, d, s, t):
        if s + t < half or (s + t == half and u == d):
            send(kv_at(u, d, s), z_by(d, t), "kv z", u, d, s + t, dst=kv_at(u, d, s + t))

    def qo_at(d, s):
        if s == half:
            return qo_weights.at[x, c, d, slot(d, s)]
        return qo_weights.at[x, c, :, slot(d, s)]

    def qo_pass(d, s, t):
        if s + t <= half:
            row = d if s + t == half else slice(None)
            src = qo_weights.at[x, c, row, slot(d, s)]
            send(src, z_by(d, t), "qo z", d, s + t, dst=qo_at(d, s + t))

    def normalize(first, last):
        def norm_step(i, carry):
            at = pl.ds(pl.multiple_of(i * NORM_ROWS, NORM_ROWS), NORM_ROWS)
            full = raw[at, :].astype(jnp.float32)
            centered = full - jnp.mean(full, axis=-1, keepdims=True)
            spread = jnp.mean(centered * centered, axis=-1, keepdims=True)
            scaled = centered * lax.rsqrt(spread + 1e-06)
            normed[at, :] = (scaled * (1.0 + mod[0:1, :]) + mod[1:2, :]).astype(jnp.bfloat16)
            return carry

        lax.fori_loop(first // NORM_ROWS, last // NORM_ROWS, norm_step, 0)

    def accumulate(first, places):
        lhs = jnp.concatenate([normed[:, column(row, at)] for row, at in places], axis=1)
        for u in (KEY, VALUE):
            rhs = jnp.concatenate(
                [kv_weights[:, row, at, u].reshape(2 * ROWS, WIDTH) for row, at in places], axis=0
            )
            part = jnp.dot(lhs, rhs, preferred_element_type=jnp.float32)
            if first:
                acc[:, u * WIDTH : (u + 1) * WIDTH] = part
            else:
                acc[:, u * WIDTH : (u + 1) * WIDTH] += part

    def places_of(row, g):
        a, b = slots[g]
        arrived(kv_weights.at[1 - c, row, a:b], sibling, "kv s", row, g)
        return [(row, at) for at in range(a, b)]

    def stage_parts(g, d):
        odd = 2 * g + 1
        at = slot(d, odd)
        if odd + 1 < half:
            return [(slice(at, at + 2), slice(None))]
        return [(slice(at, at + 1), slice(None)), (slice(2 * half - 1, 2 * half), slice(d, d + 1))]

    def across(g):
        for d in (0, 1):
            for i, (at, u) in enumerate(stage_parts(g, d)):
                ref, dst = kv_weights.at[c, 0, at, u], kv_weights.at[c, 1, at, u]
                send(ref, y_next[d], "kv y", g, d, i, dst=dst)

    def from_across(g):
        for d in (0, 1):
            if g == 0:
                arrived(kv_weights.at[c, 1, 0, d], y_next[1 - d], "kv y own", d)
            for i, (at, u) in enumerate(stage_parts(g, d)):
                arrived(kv_weights.at[c, 1, at, u], y_next[1 - d], "kv y", g, d, i)
        a, b = slots[g]
        send(kv_weights.at[c, 1, a:b], sibling, "kv s", 1, g)

    def qo_across_x(g):
        a, b = slots[g]
        for d in (0, 1):
            send(qo_weights.at[x, c, :, a:b], x_next[d], "qo x", g, d)

    def qo_relay_x(g):
        a, b = slots[g]
        for d in (0, 1):
            arrived(qo_weights.at[x_at[1 - d], c, :, a:b], x_next[1 - d], "qo x", g, d)
            send(qo_weights.at[x_at[1 - d], c, d, a:b], x_next[d], "qo r", g, d)

    def qo_to_core(g):
        a, b = slots[g]
        for d in (0, 1):
            arrived(qo_weights.at[x_far, c, d, a:b], x_next[1 - d], "qo r", g, d)
        send(qo_weights.at[:, c, :, a:b], sibling, "qo s", g)

    loads[0].wait()
    loads[1].wait()
    for t in (2, 1):
        for u in (KEY, VALUE):
            for d in (0, 1):
                kv_pass(u, d, 0, t)
    for d in (0, 1):
        ref, dst = kv_weights.at[c, 0, 0, d], kv_weights.at[c, 1, 0, d]
        send(ref, y_next[d], "kv y own", d, dst=dst)
    loads[2].wait()
    loads[3].wait()
    send(qo_weights.at[x, c, 0, 0], y_next[0], "qo y", dst=qo_weights.at[x, c, 1, 0])
    loads[4].wait()
    loads[5].wait()
    loads[6].wait()
    normalize(0, BORDER)
    arrived(qo_weights.at[x, c, 1, 0], y_next[1], "qo y")
    for t in (2, 1):
        for d in (0, 1):
            qo_pass(d, 0, t)

    for g in range(stages):
        even = 2 * g + 2
        for u in (KEY, VALUE):
            for d in (0, 1):
                if even == half and u != d:
                    continue
                arrived(kv_at(u, d, even), z_by(1 - d, 2), "kv z", u, d, even)
                kv_pass(u, d, even, 2)
        for u in (KEY, VALUE):
            for d in (0, 1):
                kv_pass(u, d, even, 1)
        for u in (KEY, VALUE):
            for d in (0, 1):
                arrived(kv_at(u, d, even - 1), z_by(1 - d, 1), "kv z", u, d, even - 1)
        across(g)
        a, b = slots[g]
        send(kv_weights.at[c, 0, a:b], sibling, "kv s", 0, g)
        for d in (0, 1):
            arrived(qo_at(d, even), z_by(1 - d, 2), "qo z", d, even)
            for t in (2, 1):
                qo_pass(d, even, t)
        for d in (0, 1):
            arrived(qo_at(d, even - 1), z_by(1 - d, 1), "qo z", d, even - 1)
        qo_across_x(g)
        if g == 0:
            normalize(BORDER, rows)
        else:
            from_across(g - 1)
            qo_relay_x(g - 1)
            accumulate(g == 1, places_of(0, g - 1) + (places_of(1, g - 2) if g > 1 else []))
    last = stages - 1
    places = places_of(0, last) + (places_of(1, last - 1) if last > 0 else [])
    accumulate(last == 0, places)
    from_across(last)
    accumulate(False, places_of(1, last))

    padded[BORDER : BORDER + rows, :WIDTH] = head_norm(acc[:, :WIDTH], gain[1:2, :])
    padded[BORDER : BORDER + rows, WIDTH:] = acc[:, WIDTH:].astype(jnp.bfloat16)
    send(
        padded.at[BORDER : 2 * BORDER],
        before,
        "head",
        dst=padded.at[BORDER + rows : 2 * BORDER + rows],
    )
    send(padded.at[rows : rows + BORDER], after, "tail", dst=padded.at[0:BORDER])

    qo_relay_x(last)
    for g in range(stages):
        qo_to_core(g)
    for g in range(stages):
        a, b = slots[g]
        arrived(qo_weights.at[:, 1 - c, :, a:b], sibling, "qo s", g)

    def whole(row, at, which):
        return [qo_weights[q, core, row, at, which] for core in (0, 1) for q in range(PARTS)]

    everything = [(row, at) for row in (0, 1) for at in range(n)]
    total = jnp.zeros((rows, WIDTH), jnp.float32)
    for i in range(0, len(everything), 4):
        group = everything[i : i + 4]
        lhs = jnp.concatenate([normed[:, column(row, at)] for row, at in group], axis=1)
        rhs = jnp.concatenate([p for row, at in group for p in whole(row, at, QUERY)], axis=0)
        total = total + jnp.dot(lhs, rhs, preferred_element_type=jnp.float32)
    query[...] = head_norm(total, gain[0:1, :])

    scale = 1.0 / math.sqrt(HEAD_DIM)

    def part_of(tile, head, start, count, weight=None):
        cols = slice(head * HEAD_DIM, (head + 1) * HEAD_DIM)
        q = query[tile * TILE : (tile + 1) * TILE, cols]
        k = padded[start : start + count, cols]
        v = padded[start : start + count, WIDTH + head * HEAD_DIM : WIDTH + (head + 1) * HEAD_DIM]
        score = lax.dot_general(
            q, k, (((1,), (1,)), ((), ())), preferred_element_type=jnp.float32
        )
        raised = jnp.exp(score * scale)
        if weight is not None:
            raised = raised * weight
        low = jnp.sum(raised, axis=-1, keepdims=True)
        high = jnp.dot(raised.astype(jnp.bfloat16), v, preferred_element_type=jnp.float32)
        return high, jnp.broadcast_to(low, (TILE, HEAD_DIM))

    for tile in range(tiles):
        for head in range(HEADS):
            high, low = part_of(tile, head, BORDER, rows)
            top[tile, head] = high
            bottom[tile, head] = low

    arrived(padded.at[0:BORDER], before, "tail")
    arrived(padded.at[BORDER + rows : 2 * BORDER + rows], after, "head")
    has_before = jnp.where(frame > 0, 1.0, 0.0)
    has_after = jnp.where(frame < nx * nyh - 1, 1.0, 0.0)
    for tile in range(tiles):
        done = []
        for head in range(HEADS):
            high, low = top[tile, head], bottom[tile, head]
            first, end = tile * TILE, (tile + 5) * TILE
            if first < BORDER:
                more, less = part_of(tile, head, first, BORDER - first, has_before)
                high, low = high + more, low + less
            if end > BORDER + rows:
                more, less = part_of(tile, head, BORDER + rows, end - BORDER - rows, has_after)
                high, low = high + more, low + less
            done.append((high / low).astype(jnp.bfloat16))
        attended[tile * TILE : (tile + 1) * TILE, :] = jnp.concatenate(done, axis=1)

    stored = []
    for i in range(0, len(everything), 2):
        pair = everything[i : i + 2]
        rhs = jnp.concatenate([p for row, at in pair for p in whole(row, at, OUT)], axis=0)
        part = lax.dot_general(
            attended[...], rhs, (((1,), (1,)), ((), ())), preferred_element_type=jnp.float32
        ).astype(jnp.bfloat16)
        for j, (row, at) in enumerate(pair):
            result[i + j] = part[:, j * 2 * ROWS : (j + 1) * 2 * ROWS]
            copy = pltpu.make_async_copy(
                result.at[i + j], mixed.at[:, column(row, at)], out_sems.at[i + j]
            )
            copy.start()
            stored.append(copy)
    for copy in stored:
        copy.wait()
    for copy in sent:
        copy.wait_send()


def on_device(sizes, frames, modulation, w_qkv, qk_gain, w_out):
    n = sizes[0]
    rows, features = frames.shape[1:]
    anywhere = pl.BlockSpec(memory_space=pl.ANY)
    mixed = pl.pallas_call(
        functools.partial(kernel, sizes, Counter()),
        out_shape=jax.ShapeDtypeStruct((rows, features), jnp.bfloat16),
        in_specs=[anywhere] * 5,
        out_specs=anywhere,
        scratch_shapes=[
            pltpu.VMEM((2, 2, n, 2, ROWS, WIDTH), jnp.bfloat16),
            pltpu.VMEM((PARTS, 2, 2, n, 2, PIECE, WIDTH), jnp.bfloat16),
            pltpu.VMEM((rows, features), jnp.bfloat16),
            pltpu.VMEM((rows, features), jnp.bfloat16),
            pltpu.VMEM((2, features), jnp.float32),
            pltpu.VMEM((2, HEAD_DIM), jnp.float32),
            pltpu.VMEM((rows, 2 * WIDTH), jnp.float32),
            pltpu.VMEM((rows + 2 * BORDER, 2 * WIDTH), jnp.bfloat16),
            pltpu.VMEM((rows, WIDTH), jnp.bfloat16),
            pltpu.VMEM((rows // TILE, HEADS, TILE, HEAD_DIM), jnp.float32),
            pltpu.VMEM((rows // TILE, HEADS, TILE, HEAD_DIM), jnp.float32),
            pltpu.VMEM((rows, WIDTH), jnp.bfloat16),
            pltpu.VMEM((2 * n, rows, 2 * ROWS), jnp.bfloat16),
            pltpu.SemaphoreType.DMA((7,)),
            pltpu.SemaphoreType.DMA((96,)),
            pltpu.SemaphoreType.DMA((96,)),
            pltpu.SemaphoreType.DMA((2 * n,)),
        ],
        compiler_params=pltpu.CompilerParams(collective_id=0, has_side_effects=True),
    )(frames[0], modulation[0], w_qkv, qk_gain, jnp.transpose(w_out))
    return mixed[None]


def solution(mesh, n=12, nx=4, nyh=4):
    finer = Mesh(mesh.devices.reshape(2, n, 2, nx, nyh), AXES)
    fsdp, frame = ("yl", "z", "c"), ("x", "yh")
    placed = (P(fsdp, frame, None), P(fsdp, None, None), P(fsdp, None), P(), P(None, fsdp))
    return jax.shard_map(
        functools.partial(on_device, (n, nx, nyh)),
        mesh=finer,
        in_specs=placed,
        out_specs=P(fsdp, frame, None),
        check_vma=False,
    )
```

```python
import functools
import math

import jax
import jax.numpy as jnp
from jax import lax
from jax.experimental import pallas as pl
from jax.experimental.pallas import tpu as pltpu
from jax.sharding import Mesh
from jax.sharding import PartitionSpec as P

HEAD_DIM = 128
HEADS = 2
TILE = 128
BORDER = 256
WIDTH = HEADS * HEAD_DIM
ROWS = 64
MESH = pl.DeviceIdType.MESH
AXES = ("yl", "z", "c", "x", "yh")
KEY, VALUE = 0, 1
QUERY, OUT = 0, 1
PARTS = 4
PIECE = ROWS // PARTS
NORM_ROWS = 16


class Counter:
    def __init__(self):
        self.ids = {}

    def __call__(self, *key):
        return self.ids.setdefault(key, len(self.ids))


def head_norm(block, gain):
    parts = []
    for head in range(HEADS):
        part = block[:, head * HEAD_DIM : (head + 1) * HEAD_DIM]
        squares = jnp.mean(part * part, axis=-1, keepdims=True)
        parts.append(part * lax.rsqrt(squares + 1e-06) * gain)
    return jnp.concatenate(parts, axis=1).astype(jnp.bfloat16)


def stage_slots(half):
    bounds = [0, 5] if half > 2 else [0, 4]
    while bounds[-1] < 2 * half:
        bounds.append(min(bounds[-1] + 4, 2 * half))
    return list(zip(bounds[:-1], bounds[1:]))


def kernel(
    sizes,
    copies,
    frames,
    modulation,
    w_qkv,
    qk_gain,
    w_out_t,
    attended,
    out_rows,
    kv_weights,
    qo_weights,
    raw,
    normed,
    mod,
    gain,
    acc,
    keys,
    values,
    query,
    top,
    bottom,
    shares,
    local_sems,
    send_sems,
    recv_sems,
):
    n, nx, nyh = sizes
    half = n // 2
    stages = half // 2
    slots = stage_slots(half)
    rows = raw.shape[0]
    tiles = rows // TILE
    yl, z, c = lax.axis_index("yl"), lax.axis_index("z"), lax.axis_index("c")
    x, yh = lax.axis_index("x"), lax.axis_index("yh")
    other = 1 - yl
    frame = x * nyh + yh

    def z_by(d, t):
        return {"z": lax.rem(z + (t if d == 0 else n - t), n)}

    y_next = [
        {"yl": other, "yh": lax.rem(yh + yl, nyh)},
        {"yl": other, "yh": lax.rem(yh + nyh - other, nyh)},
    ]
    x_at = [lax.rem(x + 1, nx), lax.rem(x + nx - 1, nx)]
    x_next = [{"x": x_at[0]}, {"x": x_at[1]}]
    x_far = lax.rem(x + 2, nx)
    sibling = {"c": 1 - c}
    after = {"yh": lax.rem(yh + 1, nyh), "x": lax.rem(x + (yh + 1) // nyh, nx)}
    before = {
        "yh": lax.rem(yh + nyh - 1, nyh),
        "x": lax.rem(x + nx - 1 + (yh + nyh - 1) // nyh, nx),
    }

    def slot(d, s):
        if s == 0:
            return 0
        base = 1 + 4 * ((s - 1) // 2)
        if s >= half - 1:
            return base + (d if s < half else 2)
        return base + 2 * d + (s - 1) % 2

    offset = {0: 0}
    for d in (0, 1):
        for s in range(1, half + 1):
            offset[slot(d, s)] = -s if d == 0 else s

    def column(row, at):
        start = ((yl if row == 0 else other) * n + lax.rem(z + n + offset[at], n)) * 2 * ROWS
        return pl.ds(pl.multiple_of(start, 2 * ROWS), 2 * ROWS)

    def local(src, dst, i):
        copy = pltpu.make_async_copy(src, dst, local_sems.at[i])
        copy.start()
        return copy

    piece = pl.ds(pl.multiple_of(x * PIECE, PIECE), PIECE)
    loads = [
        local(w_qkv.at[:, WIDTH : 2 * WIDTH], kv_weights.at[c, 0, KEY, 0], 0),
        local(w_qkv.at[:, 2 * WIDTH :], kv_weights.at[c, 0, VALUE, 0], 1),
        local(w_qkv.at[piece, :WIDTH], qo_weights.at[x, c, 0, 0, QUERY], 2),
        local(w_out_t.at[piece, :], qo_weights.at[x, c, 0, 0, OUT], 3),
        local(modulation, mod, 4),
        local(qk_gain, gain, 5),
        local(frames, raw, 6),
    ]

    sent = []

    def remote(src, dst, to, *key):
        i = copies(*key)
        return pltpu.make_async_remote_copy(
            src, dst, send_sems.at[i], recv_sems.at[i], device_id=to, device_id_type=MESH
        )

    def send(ref, to, *key, dst=None):
        copy = remote(ref, ref if dst is None else dst, to, *key)
        copy.start()
        sent.append(copy)

    def arrived(ref, to, *key):
        remote(ref, ref, to, *key).wait_recv()

    barrier = pltpu.get_barrier_semaphore()
    partners = [z_by(d, t) for d in (0, 1) for t in (1, 2)]
    partners += [*y_next, *x_next, sibling, after, before]
    for to in partners:
        pl.semaphore_signal(barrier, inc=1, device_id=to, device_id_type=MESH)
    pl.semaphore_wait(barrier, len(partners))

    def kv_at(u, d, s):
        return kv_weights.at[c, 0, u, slot(d, s)]

    def kv_pass(u, d, s, t):
        if s + t < half or (s + t == half and u == d):
            send(kv_at(u, d, s), z_by(d, t), "kv z", u, d, s + t, dst=kv_at(u, d, s + t))

    def qo_at(d, s):
        if s == half:
            return qo_weights.at[x, c, d, slot(d, s)]
        return qo_weights.at[x, c, :, slot(d, s)]

    def qo_pass(d, s, t):
        if s + t <= half:
            row = d if s + t == half else slice(None)
            src = qo_weights.at[x, c, row, slot(d, s)]
            send(src, z_by(d, t), "qo z", d, s + t, dst=qo_at(d, s + t))

    def normalize(first, last):
        def norm_step(i, carry):
            at = pl.ds(pl.multiple_of(i * NORM_ROWS, NORM_ROWS), NORM_ROWS)
            full = raw[at, :].astype(jnp.float32)
            centered = full - jnp.mean(full, axis=-1, keepdims=True)
            spread = jnp.mean(centered * centered, axis=-1, keepdims=True)
            scaled = centered * lax.rsqrt(spread + 1e-06)
            normed[at, :] = (scaled * (1.0 + mod[0:1, :]) + mod[1:2, :]).astype(jnp.bfloat16)
            return carry

        lax.fori_loop(first // NORM_ROWS, last // NORM_ROWS, norm_step, 0)

    def accumulate(u, first, places):
        lhs = jnp.concatenate([normed[:, column(row, at)] for row, at in places], axis=1)
        rhs = jnp.concatenate(
            [kv_weights[:, row, u, at].reshape(2 * ROWS, WIDTH) for row, at in places], axis=0
        )
        part = jnp.dot(lhs, rhs, preferred_element_type=jnp.float32)
        if first:
            acc[u] = part
        else:
            acc[u] += part

    def places_of(u, row, g):
        a, b = slots[g]
        arrived(kv_weights.at[1 - c, row, u, a:b], sibling, "kv s", u, row, g)
        return [(row, at) for at in range(a, b)]

    def stage_parts(u, g, d):
        odd = 2 * g + 1
        at = slot(d, odd)
        if odd + 1 < half:
            return [slice(at, at + 2)]
        return [slice(at, at + 1)] + ([slice(2 * half - 1, 2 * half)] if u == d else [])

    def across(u, g):
        for d in (0, 1):
            for i, at in enumerate(stage_parts(u, g, d)):
                ref, dst = kv_weights.at[c, 0, u, at], kv_weights.at[c, 1, u, at]
                send(ref, y_next[d], "kv y", u, g, d, i, dst=dst)

    def from_across(u, g):
        if g == 0:
            arrived(kv_weights.at[c, 1, u, 0], y_next[1 - u], "kv y own", u)
        for d in (0, 1):
            for i, at in enumerate(stage_parts(u, g, d)):
                arrived(kv_weights.at[c, 1, u, at], y_next[1 - d], "kv y", u, g, d, i)
        a, b = slots[g]
        send(kv_weights.at[c, 1, u, a:b], sibling, "kv s", u, 1, g)

    def qo_across_x(g):
        a, b = slots[g]
        for d in (0, 1):
            send(qo_weights.at[x, c, :, a:b], x_next[d], "qo x", g, d)

    def qo_relay_x(g):
        a, b = slots[g]
        for d in (0, 1):
            arrived(qo_weights.at[x_at[1 - d], c, :, a:b], x_next[1 - d], "qo x", g, d)
            send(qo_weights.at[x_at[1 - d], c, d, a:b], x_next[d], "qo r", g, d)

    def qo_to_core(g):
        a, b = slots[g]
        for d in (0, 1):
            arrived(qo_weights.at[x_far, c, d, a:b], x_next[1 - d], "qo r", g, d)
        send(qo_weights.at[:, c, :, a:b], sibling, "qo s", g)

    def qo_arrive(g):
        even = 2 * g + 2
        for d in (0, 1):
            arrived(qo_at(d, even), z_by(1 - d, 2), "qo z", d, even)
            for t in (2, 1):
                qo_pass(d, even, t)
        for d in (0, 1):
            arrived(qo_at(d, even - 1), z_by(1 - d, 1), "qo z", d, even - 1)
        qo_across_x(g)

    for u in (KEY, VALUE):
        loads[u].wait()
        for t in (2, 1):
            for d in (0, 1):
                kv_pass(u, d, 0, t)
        ref, dst = kv_weights.at[c, 0, u, 0], kv_weights.at[c, 1, u, 0]
        send(ref, y_next[u], "kv y own", u, dst=dst)
    loads[2].wait()
    loads[3].wait()
    send(qo_weights.at[x, c, 0, 0], y_next[0], "qo y", dst=qo_weights.at[x, c, 1, 0])
    loads[4].wait()
    loads[5].wait()
    loads[6].wait()
    normalize(0, BORDER)
    arrived(qo_weights.at[x, c, 1, 0], y_next[1], "qo y")
    for t in (2, 1):
        for d in (0, 1):
            qo_pass(d, 0, t)

    for g in range(stages):
        even = 2 * g + 2
        a, b = slots[g]
        for u in (KEY, VALUE):
            both = (0, 1) if even < half else (u,)
            for d in both:
                arrived(kv_at(u, d, even), z_by(1 - d, 2), "kv z", u, d, even)
                kv_pass(u, d, even, 2)
            for d in (0, 1):
                kv_pass(u, d, even, 1)
            for d in (0, 1):
                arrived(kv_at(u, d, even - 1), z_by(1 - d, 1), "kv z", u, d, even - 1)
            across(u, g)
            send(kv_weights.at[c, 0, u, a:b], sibling, "kv s", u, 0, g)
        if g == 0:
            normalize(BORDER, rows)
        else:
            for u in (KEY, VALUE):
                from_across(u, g - 1)
            qo_arrive(g - 1)
            if g > 1:
                qo_relay_x(g - 2)
            for u in (KEY, VALUE):
                places = places_of(u, 0, g - 1)
                if g > 1:
                    places += places_of(u, 1, g - 2)
                accumulate(u, g == 1, places)
    last = stages - 1
    for u in (KEY, VALUE):
        places = places_of(u, 0, last)
        if last > 0:
            places += places_of(u, 1, last - 1)
        accumulate(u, last == 0, places)
    for u in (KEY, VALUE):
        from_across(u, last)
    for u, name in ((KEY, "keys"), (VALUE, "values")):
        accumulate(u, False, places_of(u, 1, last))
        if u == KEY:
            local_rows = head_norm(acc[KEY], gain[1:2, :])
        else:
            local_rows = acc[VALUE].astype(jnp.bfloat16)
        held = keys if u == KEY else values
        held[BORDER : BORDER + rows, :] = local_rows
        ends = held.at[BORDER + rows : 2 * BORDER + rows]
        send(held.at[BORDER : 2 * BORDER], before, name + " head", dst=ends)
        send(held.at[rows : rows + BORDER], after, name + " tail", dst=held.at[0:BORDER])
        if u == KEY:
            qo_arrive(last)
            if last > 0:
                qo_relay_x(last - 1)

    qo_relay_x(last)
    for g in range(last):
        qo_to_core(g)

    def whole(row, at, which):
        return [qo_weights[q, core, row, at, which] for core in (0, 1) for q in range(PARTS)]

    def project(g_first, g_last, total):
        places = []
        for g in range(g_first, g_last):
            a, b = slots[g]
            arrived(qo_weights.at[:, 1 - c, :, a:b], sibling, "qo s", g)
            places += [(row, at) for row in (0, 1) for at in range(a, b)]
        for i in range(0, len(places), 6):
            group = places[i : i + 6]
            lhs = jnp.concatenate([normed[:, column(row, at)] for row, at in group], axis=1)
            rhs = jnp.concatenate([p for row, at in group for p in whole(row, at, QUERY)], axis=0)
            total = total + jnp.dot(lhs, rhs, preferred_element_type=jnp.float32)
        return total

    everything = [(row, at) for row in (0, 1) for at in range(n)]
    total = project(0, last, jnp.zeros((rows, WIDTH), jnp.float32))
    qo_to_core(last)
    total = project(last, stages, total)
    query[...] = head_norm(total, gain[0:1, :])

    scale = 1.0 / math.sqrt(HEAD_DIM)

    def raised_of(tile, head, start, count):
        cols = slice(head * HEAD_DIM, (head + 1) * HEAD_DIM)
        q = query[tile * TILE : (tile + 1) * TILE, cols]
        k = keys[start : start + count, cols]
        score = lax.dot_general(
            q, k, (((1,), (1,)), ((), ())), preferred_element_type=jnp.float32
        )
        return jnp.exp(score * scale)

    def mixed_values(share, head, start, count):
        v = values[start : start + count, head * HEAD_DIM : (head + 1) * HEAD_DIM]
        return jnp.dot(share, v, preferred_element_type=jnp.float32)

    for tile in range(tiles):
        for head in range(HEADS):
            raised = raised_of(tile, head, BORDER, rows)
            low = jnp.sum(raised, axis=-1, keepdims=True)
            bottom[tile, head] = jnp.broadcast_to(low, (TILE, HEAD_DIM))
            top[tile, head] = mixed_values(raised.astype(jnp.bfloat16), head, BORDER, rows)

    for row, at in everything:
        out_rows[column(row, at), :] = jnp.concatenate(whole(row, at, OUT), axis=0)

    def wait_border(held, name):
        arrived(held.at[0:BORDER], before, name + " tail")
        arrived(held.at[BORDER + rows : 2 * BORDER + rows], after, name + " head")

    def far_parts(tile):
        first, end = tile * TILE, (tile + 5) * TILE
        found, at = [], 0
        for start, stop, weight in (
            (first, BORDER, has_before),
            (BORDER + rows, end, has_after),
        ):
            if stop > start:
                found.append((start, stop - start, at, weight))
                at += stop - start
        return found

    has_before = jnp.where(frame > 0, 1.0, 0.0)
    has_after = jnp.where(frame < nx * nyh - 1, 1.0, 0.0)
    wait_border(keys, "keys")
    for tile in range(tiles):
        for head in range(HEADS):
            for start, count, at, weight in far_parts(tile):
                raised = raised_of(tile, head, start, count) * weight
                low = jnp.sum(raised, axis=-1, keepdims=True)
                bottom[tile, head] += jnp.broadcast_to(low, (TILE, HEAD_DIM))
                shares[tile, head, :, at : at + count] = raised.astype(jnp.bfloat16)
    wait_border(values, "values")
    for tile in range(tiles):
        done = []
        for head in range(HEADS):
            high = top[tile, head]
            for start, count, at, _ in far_parts(tile):
                share = shares[tile, head, :, at : at + count]
                high = high + mixed_values(share, head, start, count)
            done.append((high / bottom[tile, head]).astype(jnp.bfloat16))
        attended[tile * TILE : (tile + 1) * TILE, :] = jnp.concatenate(done, axis=1)

    for copy in sent:
        copy.wait_send()


def on_device(sizes, frames, modulation, w_qkv, qk_gain, w_out):
    n = sizes[0]
    rows, features = frames.shape[1:]
    anywhere = pl.BlockSpec(memory_space=pl.ANY)
    attended, out_rows = pl.pallas_call(
        functools.partial(kernel, sizes, Counter()),
        out_shape=(
            pltpu.VMEM((rows, WIDTH), jnp.bfloat16),
            pltpu.VMEM((features, WIDTH), jnp.bfloat16),
        ),
        in_specs=[anywhere] * 5,
        out_specs=(pl.BlockSpec(memory_space=pltpu.VMEM),) * 2,
        scratch_shapes=[
            pltpu.VMEM((2, 2, 2, n, ROWS, WIDTH), jnp.bfloat16),
            pltpu.VMEM((PARTS, 2, 2, n, 2, PIECE, WIDTH), jnp.bfloat16),
            pltpu.VMEM((rows, features), jnp.bfloat16),
            pltpu.VMEM((rows, features), jnp.bfloat16),
            pltpu.VMEM((2, features), jnp.float32),
            pltpu.VMEM((2, HEAD_DIM), jnp.float32),
            pltpu.VMEM((2, rows, WIDTH), jnp.float32),
            pltpu.VMEM((rows + 2 * BORDER, WIDTH), jnp.bfloat16),
            pltpu.VMEM((rows + 2 * BORDER, WIDTH), jnp.bfloat16),
            pltpu.VMEM((rows, WIDTH), jnp.bfloat16),
            pltpu.VMEM((rows // TILE, HEADS, TILE, HEAD_DIM), jnp.float32),
            pltpu.VMEM((rows // TILE, HEADS, TILE, HEAD_DIM), jnp.float32),
            pltpu.VMEM((rows // TILE, HEADS, TILE, BORDER), jnp.bfloat16),
            pltpu.SemaphoreType.DMA((7,)),
            pltpu.SemaphoreType.DMA((112,)),
            pltpu.SemaphoreType.DMA((112,)),
        ],
        compiler_params=pltpu.CompilerParams(collective_id=0, has_side_effects=True),
    )(frames[0], modulation[0], w_qkv, qk_gain, jnp.transpose(w_out))
    mixed = lax.dot_general(
        attended, out_rows, (((1,), (1,)), ((), ())), preferred_element_type=jnp.float32
    )
    return mixed.astype(jnp.bfloat16)[None]


def solution(mesh, n=12, nx=4, nyh=4):
    finer = Mesh(mesh.devices.reshape(2, n, 2, nx, nyh), AXES)
    fsdp, frame = ("yl", "z", "c"), ("x", "yh")
    placed = (P(fsdp, frame, None), P(fsdp, None, None), P(fsdp, None), P(), P(None, fsdp))
    return jax.shard_map(
        functools.partial(on_device, (n, nx, nyh)),
        mesh=finer,
        in_specs=placed,
        out_specs=P(fsdp, frame, None),
        check_vma=False,
    )
```

```python
import functools
import math

import jax
import jax.numpy as jnp
from jax import lax
from jax.experimental import pallas as pl
from jax.experimental.pallas import tpu as pltpu
from jax.sharding import Mesh
from jax.sharding import PartitionSpec as P

HEAD_DIM = 128
HEADS = 2
TILE = 128
BORDER = 256
WIDTH = HEADS * HEAD_DIM
ROWS = 64
MESH = pl.DeviceIdType.MESH
AXES = ("yl", "z", "c", "x", "yh")
KEY, VALUE = 0, 1
QUERY, OUT = 0, 1
PARTS = 4
PIECE = ROWS // PARTS
NORM_ROWS = 16


class Counter:
    def __init__(self):
        self.ids = {}

    def __call__(self, *key):
        return self.ids.setdefault(key, len(self.ids))


def head_norm(block, gain):
    parts = []
    for head in range(HEADS):
        part = block[:, head * HEAD_DIM : (head + 1) * HEAD_DIM]
        squares = jnp.mean(part * part, axis=-1, keepdims=True)
        parts.append(part * lax.rsqrt(squares + 1e-06) * gain)
    return jnp.concatenate(parts, axis=1).astype(jnp.bfloat16)


def stage_slots(half):
    bounds = [0, 5] if half > 2 else [0, 4]
    while bounds[-1] < 2 * half:
        bounds.append(min(bounds[-1] + 4, 2 * half))
    return list(zip(bounds[:-1], bounds[1:]))


def kernel(
    sizes,
    copies,
    frames,
    modulation,
    w_qkv,
    qk_gain,
    w_out_t,
    attended,
    out_rows,
    kv_weights,
    qo_weights,
    raw,
    normed,
    mod,
    gain,
    acc,
    keys,
    values,
    query,
    top,
    bottom,
    shares,
    local_sems,
    send_sems,
    recv_sems,
):
    n, nx, nyh = sizes
    half = n // 2
    stages = half // 2
    slots = stage_slots(half)
    rows = raw.shape[0]
    tiles = rows // TILE
    yl, z, c = lax.axis_index("yl"), lax.axis_index("z"), lax.axis_index("c")
    x, yh = lax.axis_index("x"), lax.axis_index("yh")
    other = 1 - yl
    frame = x * nyh + yh

    def z_by(d, t):
        return {"z": lax.rem(z + (t if d == 0 else n - t), n)}

    y_next = [
        {"yl": other, "yh": lax.rem(yh + yl, nyh)},
        {"yl": other, "yh": lax.rem(yh + nyh - other, nyh)},
    ]
    x_at = [lax.rem(x + 1, nx), lax.rem(x + nx - 1, nx)]
    x_next = [{"x": x_at[0]}, {"x": x_at[1]}]
    x_far = lax.rem(x + 2, nx)
    sibling = {"c": 1 - c}
    after = {"yh": lax.rem(yh + 1, nyh), "x": lax.rem(x + (yh + 1) // nyh, nx)}
    before = {
        "yh": lax.rem(yh + nyh - 1, nyh),
        "x": lax.rem(x + nx - 1 + (yh + nyh - 1) // nyh, nx),
    }

    def slot(d, s):
        if s == 0:
            return 0
        base = 1 + 4 * ((s - 1) // 2)
        if s >= half - 1:
            return base + (d if s < half else 2)
        return base + 2 * d + (s - 1) % 2

    offset = {0: 0}
    for d in (0, 1):
        for s in range(1, half + 1):
            offset[slot(d, s)] = -s if d == 0 else s

    def column(row, at):
        start = ((yl if row == 0 else other) * n + lax.rem(z + n + offset[at], n)) * 2 * ROWS
        return pl.ds(pl.multiple_of(start, 2 * ROWS), 2 * ROWS)

    def local(src, dst, i):
        copy = pltpu.make_async_copy(src, dst, local_sems.at[i])
        copy.start()
        return copy

    piece = pl.ds(pl.multiple_of(x * PIECE, PIECE), PIECE)
    loads = [
        local(w_qkv.at[:, WIDTH : 2 * WIDTH], kv_weights.at[c, 0, KEY, 0], 0),
        local(w_qkv.at[:, 2 * WIDTH :], kv_weights.at[c, 0, VALUE, 0], 1),
        local(w_qkv.at[piece, :WIDTH], qo_weights.at[x, c, 0, 0, QUERY], 2),
        local(w_out_t.at[piece, :], qo_weights.at[x, c, 0, 0, OUT], 3),
        local(modulation, mod, 4),
        local(qk_gain, gain, 5),
        local(frames, raw, 6),
    ]

    sent = []

    def remote(src, dst, to, *key):
        i = copies(*key)
        return pltpu.make_async_remote_copy(
            src, dst, send_sems.at[i], recv_sems.at[i], device_id=to, device_id_type=MESH
        )

    def send(ref, to, *key, dst=None):
        copy = remote(ref, ref if dst is None else dst, to, *key)
        copy.start()
        sent.append(copy)

    def arrived(ref, to, *key):
        remote(ref, ref, to, *key).wait_recv()

    barrier = pltpu.get_barrier_semaphore()
    partners = [z_by(d, t) for d in (0, 1) for t in (1, 2)]
    partners += [*y_next, *x_next, sibling, after, before]
    for to in partners:
        pl.semaphore_signal(barrier, inc=1, device_id=to, device_id_type=MESH)
    pl.semaphore_wait(barrier, len(partners))

    def kv_at(u, d, s):
        return kv_weights.at[c, 0, u, slot(d, s)]

    def kv_pass(u, d, s, t):
        if s + t < half or (s + t == half and u == d):
            send(kv_at(u, d, s), z_by(d, t), "kv z", u, d, s + t, dst=kv_at(u, d, s + t))

    def qo_at(d, s):
        if s == half:
            return qo_weights.at[x, c, d, slot(d, s)]
        return qo_weights.at[x, c, :, slot(d, s)]

    def qo_pass(d, s, t):
        if s + t <= half:
            row = d if s + t == half else slice(None)
            src = qo_weights.at[x, c, row, slot(d, s)]
            send(src, z_by(d, t), "qo z", d, s + t, dst=qo_at(d, s + t))

    def normalize(first, last):
        def norm_step(i, carry):
            at = pl.ds(pl.multiple_of(i * NORM_ROWS, NORM_ROWS), NORM_ROWS)
            full = raw[at, :].astype(jnp.float32)
            centered = full - jnp.mean(full, axis=-1, keepdims=True)
            spread = jnp.mean(centered * centered, axis=-1, keepdims=True)
            scaled = centered * lax.rsqrt(spread + 1e-06)
            normed[at, :] = (scaled * (1.0 + mod[0:1, :]) + mod[1:2, :]).astype(jnp.bfloat16)
            return carry

        lax.fori_loop(first // NORM_ROWS, last // NORM_ROWS, norm_step, 0)

    def accumulate(u, first, places):
        lhs = jnp.concatenate([normed[:, column(row, at)] for row, at in places], axis=1)
        rhs = jnp.concatenate(
            [kv_weights[:, row, u, at].reshape(2 * ROWS, WIDTH) for row, at in places], axis=0
        )
        part = jnp.dot(lhs, rhs, preferred_element_type=jnp.float32)
        if first:
            acc[u] = part
        else:
            acc[u] += part

    def places_of(u, row, g):
        a, b = slots[g]
        arrived(kv_weights.at[1 - c, row, u, a:b], sibling, "kv s", u, row, g)
        return [(row, at) for at in range(a, b)]

    def stage_parts(u, g, d):
        odd = 2 * g + 1
        at = slot(d, odd)
        if odd + 1 < half:
            return [slice(at, at + 2)]
        return [slice(at, at + 1)] + ([slice(2 * half - 1, 2 * half)] if u == d else [])

    def across(u, g):
        for d in (0, 1):
            for i, at in enumerate(stage_parts(u, g, d)):
                ref, dst = kv_weights.at[c, 0, u, at], kv_weights.at[c, 1, u, at]
                send(ref, y_next[d], "kv y", u, g, d, i, dst=dst)

    def from_across(u, g):
        if g == 0:
            arrived(kv_weights.at[c, 1, u, 0], y_next[1 - u], "kv y own", u)
        for d in (0, 1):
            for i, at in enumerate(stage_parts(u, g, d)):
                arrived(kv_weights.at[c, 1, u, at], y_next[1 - d], "kv y", u, g, d, i)
        a, b = slots[g]
        send(kv_weights.at[c, 1, u, a:b], sibling, "kv s", u, 1, g)

    def qo_across_x(g):
        a, b = slots[g]
        for d in (0, 1):
            send(qo_weights.at[x, c, :, a:b], x_next[d], "qo x", g, d)

    def qo_relay_x(g):
        a, b = slots[g]
        for d in (0, 1):
            arrived(qo_weights.at[x_at[1 - d], c, :, a:b], x_next[1 - d], "qo x", g, d)
            send(qo_weights.at[x_at[1 - d], c, d, a:b], x_next[d], "qo r", g, d)

    def qo_to_core(g):
        a, b = slots[g]
        for d in (0, 1):
            arrived(qo_weights.at[x_far, c, d, a:b], x_next[1 - d], "qo r", g, d)
        send(qo_weights.at[:, c, :, a:b], sibling, "qo s", g)

    def qo_arrive(g):
        even = 2 * g + 2
        for d in (0, 1):
            arrived(qo_at(d, even), z_by(1 - d, 2), "qo z", d, even)
            for t in (2, 1):
                qo_pass(d, even, t)
        for d in (0, 1):
            arrived(qo_at(d, even - 1), z_by(1 - d, 1), "qo z", d, even - 1)
        qo_across_x(g)

    for u in (KEY, VALUE):
        loads[u].wait()
        for t in (2, 1):
            for d in (0, 1):
                kv_pass(u, d, 0, t)
        ref, dst = kv_weights.at[c, 0, u, 0], kv_weights.at[c, 1, u, 0]
        send(ref, y_next[u], "kv y own", u, dst=dst)
    loads[2].wait()
    loads[3].wait()
    send(qo_weights.at[x, c, 0, 0], y_next[0], "qo y", dst=qo_weights.at[x, c, 1, 0])
    loads[4].wait()
    loads[5].wait()
    loads[6].wait()
    normalize(0, BORDER)
    arrived(qo_weights.at[x, c, 1, 0], y_next[1], "qo y")
    for t in (2, 1):
        for d in (0, 1):
            qo_pass(d, 0, t)

    for g in range(stages):
        even = 2 * g + 2
        a, b = slots[g]
        for u in (KEY, VALUE):
            both = (0, 1) if even < half else (u,)
            for d in both:
                arrived(kv_at(u, d, even), z_by(1 - d, 2), "kv z", u, d, even)
                kv_pass(u, d, even, 2)
            for d in (0, 1):
                kv_pass(u, d, even, 1)
            for d in (0, 1):
                arrived(kv_at(u, d, even - 1), z_by(1 - d, 1), "kv z", u, d, even - 1)
            across(u, g)
            send(kv_weights.at[c, 0, u, a:b], sibling, "kv s", u, 0, g)
        if g == 0:
            normalize(BORDER, rows)
        else:
            for u in (KEY, VALUE):
                from_across(u, g - 1)
            qo_arrive(g - 1)
            if g > 1:
                qo_relay_x(g - 2)
            for u in (KEY, VALUE):
                places = places_of(u, 0, g - 1)
                if g > 1:
                    places += places_of(u, 1, g - 2)
                accumulate(u, g == 1, places)
    last = stages - 1
    for u in (KEY, VALUE):
        places = places_of(u, 0, last)
        if last > 0:
            places += places_of(u, 1, last - 1)
        accumulate(u, last == 0, places)
    for u in (KEY, VALUE):
        from_across(u, last)
    qo_arrive(last)
    if last > 0:
        qo_relay_x(last - 1)
    for u, name in ((KEY, "keys"), (VALUE, "values")):
        accumulate(u, False, places_of(u, 1, last))
        if u == KEY:
            local_rows = head_norm(acc[KEY], gain[1:2, :])
        else:
            local_rows = acc[VALUE].astype(jnp.bfloat16)
        held = keys if u == KEY else values
        held[BORDER : BORDER + rows, :] = local_rows
        ends = held.at[BORDER + rows : 2 * BORDER + rows]
        send(held.at[BORDER : 2 * BORDER], before, name + " head", dst=ends)
        send(held.at[rows : rows + BORDER], after, name + " tail", dst=held.at[0:BORDER])

    qo_relay_x(last)
    for g in range(last):
        qo_to_core(g)

    def whole(row, at, which):
        return [qo_weights[q, core, row, at, which] for core in (0, 1) for q in range(PARTS)]

    def project(g_first, g_last, total):
        places = []
        for g in range(g_first, g_last):
            a, b = slots[g]
            arrived(qo_weights.at[:, 1 - c, :, a:b], sibling, "qo s", g)
            places += [(row, at) for row in (0, 1) for at in range(a, b)]
        for i in range(0, len(places), 6):
            group = places[i : i + 6]
            lhs = jnp.concatenate([normed[:, column(row, at)] for row, at in group], axis=1)
            rhs = jnp.concatenate([p for row, at in group for p in whole(row, at, QUERY)], axis=0)
            total = total + jnp.dot(lhs, rhs, preferred_element_type=jnp.float32)
        return total

    everything = [(row, at) for row in (0, 1) for at in range(n)]
    total = project(0, last, jnp.zeros((rows, WIDTH), jnp.float32))
    qo_to_core(last)
    total = project(last, stages, total)
    query[...] = head_norm(total, gain[0:1, :])

    scale = 1.0 / math.sqrt(HEAD_DIM)

    def raised_of(tile, head, start, count):
        cols = slice(head * HEAD_DIM, (head + 1) * HEAD_DIM)
        q = query[tile * TILE : (tile + 1) * TILE, cols]
        k = keys[start : start + count, cols]
        score = lax.dot_general(
            q, k, (((1,), (1,)), ((), ())), preferred_element_type=jnp.float32
        )
        return jnp.exp(score * scale)

    def mixed_values(share, head, start, count):
        v = values[start : start + count, head * HEAD_DIM : (head + 1) * HEAD_DIM]
        return jnp.dot(share, v, preferred_element_type=jnp.float32)

    for tile in range(tiles):
        for head in range(HEADS):
            raised = raised_of(tile, head, BORDER, rows)
            low = jnp.sum(raised, axis=-1, keepdims=True)
            bottom[tile, head] = jnp.broadcast_to(low, (TILE, HEAD_DIM))
            top[tile, head] = mixed_values(raised.astype(jnp.bfloat16), head, BORDER, rows)

    for row, at in everything:
        out_rows[column(row, at), :] = jnp.concatenate(whole(row, at, OUT), axis=0)

    def wait_border(held, name):
        arrived(held.at[0:BORDER], before, name + " tail")
        arrived(held.at[BORDER + rows : 2 * BORDER + rows], after, name + " head")

    def far_parts(tile):
        first, end = tile * TILE, (tile + 5) * TILE
        found, at = [], 0
        for start, stop, weight in (
            (first, BORDER, has_before),
            (BORDER + rows, end, has_after),
        ):
            if stop > start:
                found.append((start, stop - start, at, weight))
                at += stop - start
        return found

    has_before = jnp.where(frame > 0, 1.0, 0.0)
    has_after = jnp.where(frame < nx * nyh - 1, 1.0, 0.0)
    wait_border(keys, "keys")
    for tile in range(tiles):
        for head in range(HEADS):
            for start, count, at, weight in far_parts(tile):
                raised = raised_of(tile, head, start, count) * weight
                low = jnp.sum(raised, axis=-1, keepdims=True)
                bottom[tile, head] += jnp.broadcast_to(low, (TILE, HEAD_DIM))
                shares[tile, head, :, at : at + count] = raised.astype(jnp.bfloat16)
    wait_border(values, "values")
    for tile in range(tiles):
        done = []
        for head in range(HEADS):
            high = top[tile, head]
            for start, count, at, _ in far_parts(tile):
                share = shares[tile, head, :, at : at + count]
                high = high + mixed_values(share, head, start, count)
            done.append((high / bottom[tile, head]).astype(jnp.bfloat16))
        attended[tile * TILE : (tile + 1) * TILE, :] = jnp.concatenate(done, axis=1)

    for copy in sent:
        copy.wait_send()


def on_device(sizes, frames, modulation, w_qkv, qk_gain, w_out):
    n = sizes[0]
    rows, features = frames.shape[1:]
    anywhere = pl.BlockSpec(memory_space=pl.ANY)
    attended, out_rows = pl.pallas_call(
        functools.partial(kernel, sizes, Counter()),
        out_shape=(
            pltpu.VMEM((rows, WIDTH), jnp.bfloat16),
            pltpu.VMEM((features, WIDTH), jnp.bfloat16),
        ),
        in_specs=[anywhere] * 5,
        out_specs=(pl.BlockSpec(memory_space=pltpu.VMEM),) * 2,
        scratch_shapes=[
            pltpu.VMEM((2, 2, 2, n, ROWS, WIDTH), jnp.bfloat16),
            pltpu.VMEM((PARTS, 2, 2, n, 2, PIECE, WIDTH), jnp.bfloat16),
            pltpu.VMEM((rows, features), jnp.bfloat16),
            pltpu.VMEM((rows, features), jnp.bfloat16),
            pltpu.VMEM((2, features), jnp.float32),
            pltpu.VMEM((2, HEAD_DIM), jnp.float32),
            pltpu.VMEM((2, rows, WIDTH), jnp.float32),
            pltpu.VMEM((rows + 2 * BORDER, WIDTH), jnp.bfloat16),
            pltpu.VMEM((rows + 2 * BORDER, WIDTH), jnp.bfloat16),
            pltpu.VMEM((rows, WIDTH), jnp.bfloat16),
            pltpu.VMEM((rows // TILE, HEADS, TILE, HEAD_DIM), jnp.float32),
            pltpu.VMEM((rows // TILE, HEADS, TILE, HEAD_DIM), jnp.float32),
            pltpu.VMEM((rows // TILE, HEADS, TILE, BORDER), jnp.bfloat16),
            pltpu.SemaphoreType.DMA((7,)),
            pltpu.SemaphoreType.DMA((112,)),
            pltpu.SemaphoreType.DMA((112,)),
        ],
        compiler_params=pltpu.CompilerParams(collective_id=0, has_side_effects=True),
    )(frames[0], modulation[0], w_qkv, qk_gain, jnp.transpose(w_out))
    mixed = lax.dot_general(
        attended, out_rows, (((1,), (1,)), ((), ())), preferred_element_type=jnp.float32
    )
    return mixed.astype(jnp.bfloat16)[None]


def solution(mesh, n=12, nx=4, nyh=4):
    finer = Mesh(mesh.devices.reshape(2, n, 2, nx, nyh), AXES)
    fsdp, frame = ("yl", "z", "c"), ("x", "yh")
    placed = (P(fsdp, frame, None), P(fsdp, None, None), P(fsdp, None), P(), P(None, fsdp))
    return jax.shard_map(
        functools.partial(on_device, (n, nx, nyh)),
        mesh=finer,
        in_specs=placed,
        out_specs=P(fsdp, frame, None),
        check_vma=False,
    )
```
